32 devices in a mesh: dp: 16 (over z, y, x), ctx: 2 (over core).
Axes of the slice: x: 2, y: 2, z: 4, core: 2. Of those that a mesh axis runs over, the one named last changes fastest.
Arguments:
- layer_in: bfloat16 [16, 256, 4096], P('dp', 'ctx'), may hold values from -6 to 6
- inner_act: bfloat16 [16, 256, 2176], P('dp', 'ctx'), may hold values from -6 to 6
- readout: bfloat16 [16, 256, 64], P('dp', 'ctx'), may hold values from -0.75 to 0.75
- w_in: bfloat16 [4096, 132], P('dp'), may hold values from -0.09375 to 0.09375
- a_log: float32 [68], replicated, may hold values from -3.9 to -1.6
- dt_bias: float32 [68], replicated, may hold values from -4 to -1
- d_skip: float32 [68], replicated, may hold values from 0.5 to 1.5
- grad_out: bfloat16 [16, 256, 2176], P('dp', 'ctx'), may hold values from -6 to 6
Outputs:
- grad_x: bfloat16 [16, 256, 2176], P('dp', 'ctx')
- grad_c: bfloat16 [16, 256, 64], P('dp', 'ctx')
- grad_proj: bfloat16 [16, 256, 132], P('dp', 'ctx')
- grad_w: float32 [4096, 132], P('dp', 'ctx')
The draws below stay inside these ranges and needn't reach their ends.
All inputs are finite; a program needn't handle non-finite values.
Results may differ from the reference program's by a relative error of at most 0.015.
Values may be sent and summed in bfloat16 or wider, within the bound.
A program may use at most 64 MiB of HBM per device.

```python
import jax
import jax.numpy as jnp
from jax import lax

D = 4096
HEADS = 68
HEADDIM = 32
STATE = 64
BLOCK = 128
SEQS = 16
LEN = 256
COLS = 132


def raised(values, stream_key, source, target, parts, factor):
    def block_of(dim):
        return (jnp.arange(values.shape[dim]) // (values.shape[dim] // parts)).reshape((-1,) + (1,) * (values.ndim - 1 - dim))

    first = jax.random.permutation(stream_key, parts)[block_of(target)]
    other_side = (block_of(target) + parts // 2) % parts
    return jnp.where((block_of(source) == first) | (block_of(source) == other_side), factor * values, values)


def block_levels(own_key, shape, shards, smallest, largest):
    level, own = 1.0, jax.random.fold_in(own_key, 6)
    for dim, blocks in shards:
        heights = jnp.exp(jax.random.uniform(jax.random.fold_in(own, dim), (blocks,), jnp.float32, smallest / len(shards), largest / len(shards)))
        level = level * jnp.repeat(heights, shape[dim] // blocks).reshape([-1 if axis == dim else 1 for axis in range(len(shape))])
    return level


def normal_values(stream_key, shape, scale, limit, shards=(), held_as=jnp.bfloat16):
    values = jax.random.normal(stream_key, shape, jnp.float32) * scale
    if len(shards) > 0:
        values = block_levels(stream_key, shape, shards, -0.22, 0.18) * values
    return jnp.clip(values, min=-limit, max=limit).astype(held_as)


def noise_with(key, shape, scale, limit, shards, heavy, dtype=jnp.bfloat16):
    array = scale * jax.random.normal(key, shape, jnp.float32)
    if shards:
        array = array * block_levels(key, shape, shards, -0.22, 0.18)
    return jnp.clip(raised(array, jax.random.fold_in(key, 3), *heavy), -limit, limit).astype(dtype)


def setup_inputs(seed: int = 0) -> dict:
    key_list = jax.random.split(jax.random.key(seed), 9)
    return {
        "layer_in": noise_with(key_list[0], (SEQS, LEN, D), 1.0, 6.0, ((0, 16), (1, 2)), (0, 2, 16, 2.0)),
        "inner_act": normal_values(key_list[1], (SEQS, LEN, HEADS * HEADDIM), 1.0, 6.0, ((0, 16), (1, 2))),
        "readout": normal_values(key_list[2], (SEQS, LEN, STATE), (STATE ** -0.5), 0.75, ((0, 16), (1, 2))),
        "w_in": normal_values(key_list[3], (D, COLS), D ** -0.5, 0.09375, ((0, 16),)),
        "a_log": jnp.clip(jax.random.uniform(key_list[4], (HEADS,), jnp.float32, -3.9, -1.6), -3.9, -1.6),
        "dt_bias": jnp.clip(jax.random.uniform(key_list[5], (HEADS,), jnp.float32, -4.0, -1.0), -4.0, -1.0),
        "d_skip": jnp.clip(jax.random.uniform(key_list[6], (HEADS,), jnp.float32, 0.5, 1.5), 0.5, 1.5),
        "grad_out": normal_values(key_list[7], (SEQS, LEN, HEADS * HEADDIM), 1.0, 6.0, ((0, 16), (1, 2))),
    }


def prepare(projected, a_log, dt_bias):
    b_rows = projected[:, :STATE].astype(jnp.bfloat16)
    step_size = jax.nn.softplus(projected[:, STATE:] + dt_bias)
    decay_rate = -jnp.exp(a_log) * step_size
    return (b_rows, step_size, decay_rate)

def blocked(values, width):
    return values.reshape(values.shape[0] // BLOCK, BLOCK, width)

def block_forward(projected, inner_rows, c_rows, a_log, dt_bias, d_skip, entry_state):
    row_count = projected.shape[0]
    head_count = a_log.shape[0]
    head_width = inner_rows.shape[1] // head_count
    block_count = row_count // BLOCK
    b_rows, step_size, decay_rate = prepare(projected, a_log, dt_bias)
    inner_blocks = inner_rows.reshape(block_count, BLOCK, head_count, head_width)
    b_blocks = blocked(b_rows, STATE)
    c_blocks = blocked(c_rows, STATE)
    step_blocks = jnp.swapaxes(blocked(step_size, head_count), 1, 2)
    cum_blocks = jnp.cumsum(jnp.swapaxes(blocked(decay_rate, head_count), 1, 2), axis=2)
    position = jnp.arange(BLOCK)
    causal = position[:, None] >= position[None, :]

    def advance(carried, pieces):
        inner_c, b_c, c_c, step_c, cum_c = pieces
        scores = jnp.dot(c_c, b_c.T, preferred_element_type=jnp.float32)
        spread = cum_c[:, :, None] - cum_c[:, None, :]
        factor = jnp.where(causal, jnp.exp(jnp.where(causal, spread, 0.0)), 0.0)
        mixing = (scores[None] * factor * step_c[:, None, :]).astype(jnp.bfloat16)
        within = jnp.einsum('hts,shp->thp', mixing.astype(jnp.float32), inner_c.astype(jnp.float32))
        to_end = jnp.exp(cum_c[:, -1:] - cum_c) * step_c
        weighted = (b_c.astype(jnp.float32)[None] * to_end[:, :, None]).astype(jnp.bfloat16)
        added = jnp.einsum('shp,hsn->hpn', inner_c.astype(jnp.float32), weighted.astype(jnp.float32))
        carried_in = jnp.einsum('tn,hpn->thp', c_c.astype(jnp.float32), carried, precision=lax.Precision.HIGHEST)
        carried_in = carried_in * jnp.exp(cum_c).T[:, :, None]
        result = (within + carried_in + d_skip[None, :, None] * inner_c.astype(jnp.float32)).astype(jnp.bfloat16)
        carried = jnp.exp(cum_c[:, -1])[:, None, None] * carried + added
        return (carried, result)
    final_state, outputs = lax.scan(advance, entry_state, (inner_blocks, b_blocks, c_blocks, step_blocks, cum_blocks))
    return (outputs.reshape(row_count, head_count * head_width), final_state)

def reference(layer_in, inner_act, readout, w_in, a_log, dt_bias, d_skip, grad_out):
    zero_state = jnp.zeros((HEADS, HEADDIM, STATE), jnp.float32)

    def per_sequence(grad_sum, pieces):
        tokens, inner_rows, c_rows, grad_rows = pieces
        projected = jnp.dot(tokens, w_in, preferred_element_type=jnp.float32)

        def forward_only(proj_val, inner_val, c_val):
            layer_out, final_state = block_forward(proj_val, inner_val, c_val, a_log, dt_bias, d_skip, zero_state)
            return layer_out
        primal, pullback = jax.vjp(forward_only, projected, inner_rows, c_rows)
        grad_p, grad_v, grad_r = pullback(grad_rows)
        proj_grad = grad_p.astype(jnp.bfloat16)
        term = lax.dot_general(tokens, proj_grad, (((0,), (0,)), ((), ())), preferred_element_type=jnp.float32)
        return (grad_sum + term, (grad_v, grad_r, proj_grad))
    start_sum = jnp.zeros((D, STATE + HEADS), jnp.float32)
    grad_sum, (grad_x, grad_c, grad_proj) = lax.scan(per_sequence, start_sum, (layer_in, inner_act, readout, grad_out))
    return (grad_x, grad_c, grad_proj, grad_sum / SEQS)
```

```python
import functools

import jax
import jax.numpy as jnp
from jax import lax
from jax.experimental import pallas as pl
from jax.experimental.pallas import tpu as pltpu
from jax.sharding import PartitionSpec as P

STATE = 64
LANES = 128
MESH = pl.DeviceIdType.MESH
F32 = jnp.float32
BF16 = jnp.bfloat16


def up(n, m):
    return -(-n // m) * m


def dot(a, b):
    return jnp.dot(a, b, preferred_element_type=F32)


def dot_nt(a, b):
    return lax.dot_general(a, b, (((1,), (1,)), ((), ())), preferred_element_type=F32)


def split(v):
    hi = v.astype(BF16)
    return hi, (v - hi.astype(F32)).astype(BF16)


def dot_split(v, b):
    hi, lo = split(v)
    return dot(hi, b) + dot(lo, b)


def dot_exact(sel, v):
    hi, rest = v.astype(BF16), None
    rest = v - hi.astype(F32)
    mid, low = split(rest)
    return dot(sel, hi) + dot(sel, mid) + dot(sel, low)


def iota(shape, dim):
    return lax.broadcasted_iota(jnp.int32, shape, dim)


def kernel(cfg, tok, x, g, c, w, vec, dexp, gx, gc, gp, gw, wall, trecv, gall, sloc, crecv, sin, gin,
           xw, gwt, dx, proj, cum_r, dt_r, cumt, rowt, qacc, ds, sv, sg, db2, dc2, gpt, part, pst, precv,
           decs, decr, gs, ws, wr, as_, ar, gsn, gr, cs, cr, ps, pr, es, er):
    n_dp, n_ctx, t, rows, heads, width, cols = cfg
    wide = rows % LANES == 0
    groups = x.shape[1] // LANES
    gh = LANES // width
    cb = cols // n_ctx
    cbp = up(cb, 8)
    me = lax.axis_index("dp")
    my = lax.axis_index("ctx")

    def peer(k):
        return lax.rem(me + k, n_dp)

    def mate(k):
        return lax.rem(my + k, n_ctx)

    def col(ref, i):
        return ref.at[:, pl.ds(pl.multiple_of(i * rows, LANES), rows)] if wide else ref.at[i]

    def blk(i):
        return pl.ds(pl.multiple_of(i * t, LANES), t)

    def lanes(q):
        return pl.ds(pl.multiple_of(q * LANES, LANES), LANES)

    barrier = pltpu.get_barrier_semaphore()

    def greet(k, carry):
        pl.semaphore_signal(barrier, inc=1, device_id=(peer(k), my), device_id_type=MESH)
        return carry

    def greet_mate(k, carry):
        pl.semaphore_signal(barrier, inc=1, device_id=(me, mate(k)), device_id_type=MESH)
        return carry

    lax.fori_loop(1, n_dp, greet, 0)
    lax.fori_loop(1, n_ctx, greet_mate, 0)
    pl.semaphore_wait(barrier, n_dp + n_ctx - 2)

    def w_copy(k):
        return pltpu.make_async_remote_copy(
            src_ref=w, dst_ref=col(wall, me), send_sem=ws.at[k], recv_sem=wr.at[k],
            device_id=(peer(k), my), device_id_type=MESH)

    def a_copy(k):
        return pltpu.make_async_remote_copy(
            src_ref=col(tok, peer(k)), dst_ref=trecv.at[blk(me), :], send_sem=as_.at[k],
            recv_sem=ar.at[k], device_id=(peer(k), my), device_id_type=MESH)

    def g_copy(k):
        return pltpu.make_async_remote_copy(
            src_ref=gpt, dst_ref=gall.at[:, blk(me)], send_sem=gsn.at[k], recv_sem=gr.at[k],
            device_id=(peer(k), my), device_id_type=MESH)

    def c_copy(k):
        other = mate(k)
        which = jnp.where(other > my, 0, 1)
        return pltpu.make_async_remote_copy(
            src_ref=sloc.at[which], dst_ref=crecv.at[my], send_sem=cs.at[k], recv_sem=cr.at[k],
            device_id=(me, other), device_id_type=MESH)

    def d_copy(k):
        return pltpu.make_async_remote_copy(
            src_ref=decs, dst_ref=decr.at[my], send_sem=es.at[k], recv_sem=er.at[k],
            device_id=(me, mate(k)), device_id_type=MESH)

    def p_copy(k):
        return pltpu.make_async_remote_copy(
            src_ref=pst.at[mate(k)], dst_ref=precv.at[my], send_sem=ps.at[k], recv_sem=pr.at[k],
            device_id=(me, mate(k)), device_id_type=MESH)

    def each(n, act):
        def step(k, carry):
            act(k)
            return carry

        lax.fori_loop(1, n, step, 0)

    each(n_dp, lambda k: w_copy(k).start())
    if wide:
        wall[:, pl.ds(pl.multiple_of(me * rows, LANES), rows)] = w[...]
        trecv[blk(me), :] = tok[:, pl.ds(pl.multiple_of(me * rows, LANES), rows)]
    else:
        wall[me] = w[...]
        trecv[blk(me), :] = tok[me]
    proj[...] = jnp.zeros_like(proj)
    qacc[...] = jnp.zeros_like(qacc)
    ds[...] = jnp.zeros_like(ds)
    for ref in (sv, sg, db2, dc2):
        ref[...] = jnp.zeros_like(ref)
    each(n_dp, lambda k: w_copy(k).wait_recv())
    each(n_dp, lambda k: a_copy(k).start())
    wcols = w.shape[0]
    if wide:
        proj[:, :wcols] = dot_nt(tok[...], wall[...])
    else:
        def shard(i, carry):
            proj[:, :wcols] += dot_nt(tok[i], wall[i])
            return carry

        lax.fori_loop(0, n_dp, shard, 0)
    rate_scale = -jnp.exp(vec[0:1, :])
    b = proj[:, :STATE].astype(BF16)
    z = proj[:, STATE:STATE + LANES] + vec[1:2, :]
    dt = jnp.maximum(z, 0.0) + jnp.log1p(jnp.exp(-jnp.abs(z)))
    row_i, col_i = iota((t, t), 0), iota((t, t), 1)
    lower = jnp.where(row_i >= col_i, 1.0, 0.0).astype(BF16)
    upper = jnp.where(col_i >= row_i, 1.0, 0.0).astype(BF16)
    cum = dot_exact(lower, rate_scale * dt)
    cum_r[...] = cum
    dt_r[...] = dt
    cumt[...] = cum.T
    last = cum_r[t - 1:t, :]
    to_end = jnp.exp(last - cum)
    wgt = to_end * dt
    grow = jnp.exp(cum)
    w_bf = wgt.astype(BF16)
    e_bf = grow.astype(BF16)
    cv = c[...]
    bt = b.astype(F32).T.astype(BF16)
    ct = cv.astype(F32).T.astype(BF16)

    def spreader(q):
        return jnp.where(iota((LANES, LANES), 0) == gh * q + iota((LANES, LANES), 1) // width, 1.0, 0.0).astype(BF16)

    def gather_heads(q):
        return jnp.where(iota((LANES, LANES), 1) == gh * q + iota((LANES, LANES), 0) // width, 1.0, 0.0).astype(BF16)

    def summary(q, carry):
        e = spreader(q)
        xq = (dot(w_bf, e) * x[:, lanes(q)].astype(F32)).astype(BF16)
        gq = (dot(e_bf, e) * g[:, lanes(q)].astype(F32)).astype(BF16)
        xw[:, lanes(q)] = xq
        gwt[:, lanes(q)] = gq
        sloc[0, :, lanes(q)] = dot(bt, xq).astype(BF16)
        sloc[1, :, lanes(q)] = dot(ct, gq).astype(BF16)
        return carry

    lax.fori_loop(0, groups, summary, 0)
    each(n_ctx, lambda k: c_copy(k).start())
    if n_ctx > 2:
        decs[...] = jnp.broadcast_to(jnp.exp(last), decs.shape)
        crecv[my] = jnp.zeros(crecv.shape[1:], BF16)
        decr[my] = jnp.zeros(decr.shape[1:], F32)
        each(n_ctx, lambda k: d_copy(k).start())

    scores = dot_nt(b, cv)
    causal = col_i >= row_i

    def mix(q, carry):
        x4, g4 = x[:, lanes(q)], g[:, lanes(q)]
        head = iota((t, LANES), 1) // width
        zero = jnp.zeros_like(x4)
        xm = jnp.concatenate([jnp.where(head == j, x4, zero) for j in range(gh)], axis=0)
        d_all = dot_nt(xm, g4)
        shift = lax.rem(LANES - gh * q, LANES)
        cum_s = pltpu.roll(cum_r[...], shift, 1)
        dt_s = pltpu.roll(dt_r[...], shift, 1)
        total = ds[...]
        quot = qacc[...]
        mixed = []
        for j in range(gh):
            h = gh * q + j
            spread = cumt[pl.ds(h, 1), :] - cum_s[:, j:j + 1]
            factor = jnp.exp(jnp.where(causal, spread, -1e30))
            step = dt_s[:, j:j + 1]
            d = d_all[j * t:(j + 1) * t]
            fs = factor * scores
            mixed.append((fs * step).astype(BF16))
            u = d * fs
            quot = jnp.where(col_i == h, jnp.sum(u, axis=1, keepdims=True), quot)
            rowt[pl.ds(h, 1), :] = jnp.sum(u * step, axis=0, keepdims=True)
            total = total + d * (factor * step)
        ds[...] = total
        qacc[...] = quot
        out = dot(jnp.concatenate(mixed, axis=0), g4)
        acc = dexp[:, lanes(q)] * g4.astype(F32)
        for j in range(gh):
            acc = acc + jnp.where(head == j, out[j * t:(j + 1) * t], 0.0)
        dx[:, lanes(q)] = acc
        return carry

    rowt[...] = jnp.zeros_like(rowt)
    lax.fori_loop(0, groups, mix, 0)
    each(n_ctx, lambda k: c_copy(k).wait_recv())
    if n_ctx > 2:
        each(n_ctx, lambda k: d_copy(k).wait_recv())
        gs[...] = jnp.zeros_like(gs)

    def apply(q, carry):
        e, et = spreader(q), gather_heads(q)
        if n_ctx == 2:
            got = crecv[1 - my, :, lanes(q)]
            none = jnp.zeros_like(got)
            s4 = jnp.where(my > 0, got, none)
            g4s = jnp.where(my < 1, got, none)
        else:
            s = jnp.zeros((STATE, LANES), F32)
            for i in range(n_ctx):
                hi, mid = split(decr[i])
                dec = (dot(hi, e) + dot(mid, e))[0:1]
                s = jnp.where(i < my, dec * s + crecv[i, :, lanes(q)].astype(F32), s)
            k = jnp.zeros((STATE, LANES), F32)
            for i in reversed(range(n_ctx)):
                hi, mid = split(decr[i])
                dec = (dot(hi, e) + dot(mid, e))[0:1]
                k = jnp.where(i > my, dec * k + crecv[i, :, lanes(q)].astype(F32), k)
            s4, g4s = s.astype(BF16), k.astype(BF16)
            both = jnp.sum(s * k, axis=0, keepdims=True)
            gs[...] += dot_split(jnp.broadcast_to(both, (8, LANES)), et)
        us = dot(cv, s4)
        ug = dot(b, g4s)
        sv[...] += dot_split(x[:, lanes(q)].astype(F32) * ug, et)
        sg[...] += dot_split(g[:, lanes(q)].astype(F32) * us, et)
        db2[...] += dot_nt(xw[:, lanes(q)], g4s)
        dc2[...] += dot_nt(gwt[:, lanes(q)], s4)
        gx[:, lanes(q)] = (dx[:, lanes(q)] + dot(w_bf, e) * ug).astype(BF16)
        return carry

    lax.fori_loop(0, groups, apply, 0)
    dsv = ds[...]
    db = dot_split(dsv, cv) + db2[...]
    dc = dot_split(dsv.T, b) + dc2[...]
    gc[...] = dc.astype(BF16)
    quot = qacc[...]
    v = sv[...]
    vw = v * wgt
    dcum = rowt[...].T + grow * sg[...] - dt * quot - vw
    tail = jnp.sum(vw, axis=0, keepdims=True)
    if n_ctx > 2:
        tail = tail + jnp.exp(last) * gs[0:1, :]
    dcum = dcum + jnp.where(row_i == t - 1, tail, 0.0)
    drate = dot_exact(upper, dcum)
    ddt = quot + v * to_end + rate_scale * drate
    dz = ddt / (1.0 + jnp.exp(-z))
    proj[...] = jnp.zeros_like(proj)
    proj[:, :STATE] = db.astype(BF16).astype(F32)
    proj[:, STATE:cols] = dz[:, :heads]
    whole = proj[...]
    gpt[...] = whole.T[:wcols].astype(BF16)
    each(n_dp, lambda k: g_copy(k).start())
    gall[:, blk(me)] = gpt[...]
    gp[...] = whole[:, :cols].astype(BF16)
    each(n_dp, lambda k: a_copy(k).wait_recv())
    each(n_dp, lambda k: g_copy(k).wait_recv())
    part[...] = dot(gall[...], trecv[...])
    for o in range(n_ctx):
        pst[o] = part[o * cb:o * cb + cbp, :]
    each(n_ctx, lambda k: p_copy(k).start())
    each(n_ctx, lambda k: p_copy(k).wait_recv())

    def add(k, acc):
        return acc + precv[mate(k)]

    total = lax.fori_loop(1, n_ctx, add, pst[my])
    gw[...] = (total * (1.0 / n_dp)).T[:, :cb]
    each(n_dp, lambda k: w_copy(k).wait_send())
    each(n_dp, lambda k: a_copy(k).wait_send())
    each(n_dp, lambda k: g_copy(k).wait_send())
    each(n_ctx, lambda k: c_copy(k).wait_send())
    each(n_ctx, lambda k: p_copy(k).wait_send())
    if n_ctx > 2:
        each(n_ctx, lambda k: d_copy(k).wait_send())


def per_device(layer_in, inner_act, readout, w_in, a_log, dt_bias, d_skip, grad_out):
    n_dp, n_ctx = lax.axis_size("dp"), lax.axis_size("ctx")
    tokens, x, c, g = layer_in[0], inner_act[0], readout[0], grad_out[0]
    t, inner = x.shape
    rows, cols = w_in.shape
    heads = a_log.shape[0]
    width = inner // heads
    wcols = up(cols, 16)
    wide = rows % LANES == 0
    wt = jnp.pad(w_in.T, ((0, wcols - cols), (0, 0)))
    if not wide:
        tokens = jnp.swapaxes(tokens.reshape(t, n_dp, rows), 0, 1)
    vec = jnp.pad(jnp.stack([a_log, dt_bias]), ((0, 6), (0, LANES - heads)))
    dexp = jnp.repeat(d_skip, width)[None]
    cb = cols // n_ctx
    cbp = up(cb, 8)
    vm = pltpu.VMEM
    scratch = [
        vm((wcols, n_dp * rows) if wide else (n_dp, wcols, rows), BF16),
        vm((n_dp * t, rows), BF16),
        vm((wcols, n_dp * t), BF16),
        vm((2, STATE, inner), BF16),
        vm((n_ctx, STATE, inner), BF16),
        vm((8, LANES), BF16),
        vm((8, LANES), BF16),
        vm((t, inner), BF16),
        vm((t, inner), BF16),
        vm((t, inner), F32),
        vm((t, 2 * LANES), F32),
        vm((t, LANES), F32),
        vm((t, LANES), F32),
        vm((LANES, t), F32),
        vm((LANES, t), F32),
        vm((t, LANES), F32),
        vm((t, t), F32),
        vm((t, LANES), F32),
        vm((t, LANES), F32),
        vm((t, STATE), F32),
        vm((t, STATE), F32),
        vm((wcols, t), BF16),
        vm((wcols, rows), F32),
        vm((n_ctx, cbp, rows), F32),
        vm((n_ctx, cbp, rows), F32),
        vm((8, LANES), F32),
        vm((n_ctx, 8, LANES), F32),
        vm((8, LANES), F32),
    ]
    dma = pltpu.SemaphoreType.DMA
    scratch += [dma((n_dp,))] * 6 + [dma((n_ctx,))] * 6
    spec = pl.BlockSpec(memory_space=pltpu.VMEM)
    cfg = (n_dp, n_ctx, t, rows, heads, width, cols)
    gx, gc, gp, gw = pl.pallas_call(
        functools.partial(kernel, cfg),
        out_shape=(
            jax.ShapeDtypeStruct((t, inner), BF16),
            jax.ShapeDtypeStruct((t, STATE), BF16),
            jax.ShapeDtypeStruct((t, cols), BF16),
            jax.ShapeDtypeStruct((rows, cb), F32),
        ),
        in_specs=[spec] * 7,
        out_specs=(spec,) * 4,
        scratch_shapes=scratch,
        compiler_params=pltpu.CompilerParams(
            collective_id=0, has_side_effects=True, vmem_limit_bytes=48 * 1024 * 1024),
        name="ssm_backward",
    )(tokens, x, g, c, wt, vec, dexp)
    return (gx[None], gc[None], gp[None], gw)


def solution(mesh):
    in_specs = (
        P("dp", "ctx", None),
        P("dp", "ctx", None),
        P("dp", "ctx", None),
        P("dp", None),
        P(),
        P(),
        P(),
        P("dp", "ctx", None),
    )
    out_specs = (P("dp", "ctx", None), P("dp", "ctx", None), P("dp", "ctx", None), P("dp", "ctx"))
    return jax.shard_map(
        per_device, mesh=mesh, in_specs=in_specs, out_specs=out_specs, check_vma=False
    )
```

```python
import functools

import jax
import jax.numpy as jnp
from jax import lax
from jax.experimental import pallas as pl
from jax.experimental.pallas import tpu as pltpu
from jax.sharding import PartitionSpec as P

STATE = 64
LANES = 128
MESH = pl.DeviceIdType.MESH
F32 = jnp.float32
BF16 = jnp.bfloat16


def inner_group(n):
    b = 1
    while b * b < n and n % (2 * b) == 0:
        b *= 2
    return b


def up(n, m):
    return -(-n // m) * m


def dot(a, b):
    return jnp.dot(a, b, preferred_element_type=F32)


def dot_nt(a, b):
    return lax.dot_general(a, b, (((1,), (1,)), ((), ())), preferred_element_type=F32)


def split(v):
    hi = v.astype(BF16)
    return hi, (v - hi.astype(F32)).astype(BF16)


def dot_split(v, b):
    hi, lo = split(v)
    return dot(hi, b) + dot(lo, b)


def dot_exact(sel, v):
    hi, rest = v.astype(BF16), None
    rest = v - hi.astype(F32)
    mid, low = split(rest)
    return dot(sel, hi) + dot(sel, mid) + dot(sel, low)


def iota(shape, dim):
    return lax.broadcasted_iota(jnp.int32, shape, dim)


def kernel(cfg, tok_h, x_h, g_h, c, w, vec, dexp, gx, gc, gp, gw, tok, x, g, wall, trecv, gall, sloc, crecv,
           dall, spread_m, gather_m, xw, gwt, dx, proj, cum_r, dt_r, cumt, rowt, qacc, ds, part, pst, precv,
           decs, decr, wzs, wzr, wfs, wfr, as_, ar, gzs, gzr, gfs, gfr, cs, cr, ps, pr, es, er, ms, mr, ls):
    n_dp, n_ctx, t, rows, heads, width, cols = cfg
    wide = rows % LANES == 0
    halved = wide and rows % (n_ctx * LANES) == 0 and n_ctx == 2
    half = rows // n_ctx
    n_b = inner_group(n_dp)
    n_a = n_dp // n_b
    my_a, my_b = lax.div(lax.axis_index("dp"), n_b), lax.rem(lax.axis_index("dp"), n_b)
    loads = [pltpu.make_async_copy(src, dst, ls.at[i]) for i, (src, dst) in enumerate(((x_h, x), (g_h, g), (tok_h, tok)))]
    for load in loads:
        load.start()
    groups = x.shape[1] // LANES
    gh = LANES // width
    cb = cols // n_ctx
    cbp = up(cb, 8)
    me = lax.axis_index("dp")
    my = lax.axis_index("ctx")

    def peer(k):
        return lax.rem(me + k, n_dp)

    def mate(k):
        return lax.rem(my + k, n_ctx)

    def col(ref, i):
        return ref.at[:, pl.ds(pl.multiple_of(i * rows, LANES), rows)] if wide else ref.at[i]

    def blk(i):
        return pl.ds(pl.multiple_of(i * t, LANES), t)

    def lanes(q):
        return pl.ds(pl.multiple_of(q * LANES, LANES), LANES)

    barrier = pltpu.get_barrier_semaphore()

    def greet(k, carry):
        pl.semaphore_signal(barrier, inc=1, device_id=(peer(k), my), device_id_type=MESH)
        return carry

    def greet_mate(k, carry):
        pl.semaphore_signal(barrier, inc=1, device_id=(me, mate(k)), device_id_type=MESH)
        return carry

    lax.fori_loop(1, n_dp, greet, 0)
    lax.fori_loop(1, n_ctx, greet_mate, 0)
    pl.semaphore_wait(barrier, n_dp + n_ctx - 2)

    def origin(ka, kb):
        return lax.rem(my_a + n_a - ka, n_a) * n_b + lax.rem(my_b + n_b - kb, n_b)

    def w_slot(i):
        if halved:
            return wall.at[my, :, pl.ds(pl.multiple_of(i * half, LANES), half)]
        return col(wall, i)

    def g_slot(i):
        return gall.at[:, blk(i)]

    def far(slot, send, recv, ka):
        return pltpu.make_async_remote_copy(
            src_ref=slot(me), dst_ref=slot(me), send_sem=send.at[ka], recv_sem=recv.at[ka],
            device_id=(lax.rem(my_a + ka, n_a) * n_b + my_b, my), device_id_type=MESH)

    def near(slot, send, recv, ka, kb):
        i = origin(ka, 0)
        return pltpu.make_async_remote_copy(
            src_ref=slot(i), dst_ref=slot(i), send_sem=send.at[ka * n_b + kb], recv_sem=recv.at[ka * n_b + kb],
            device_id=(my_a * n_b + lax.rem(my_b + kb, n_b), my), device_id_type=MESH)

    def across(ka):
        i = lax.rem(my_a + n_a - ka, n_a) * n_b
        block = wall.at[my, :, pl.ds(pl.multiple_of(i * half, LANES), n_b * half)]
        return pltpu.make_async_remote_copy(
            src_ref=block, dst_ref=block, send_sem=ms.at[ka], recv_sem=mr.at[ka],
            device_id=(me, 1 - my), device_id_type=MESH)

    def a_copy(k):
        return pltpu.make_async_remote_copy(
            src_ref=col(tok, peer(k)), dst_ref=trecv.at[blk(me), :], send_sem=as_.at[k],
            recv_sem=ar.at[k], device_id=(peer(k), my), device_id_type=MESH)

    def c_copy(k):
        other = mate(k)
        which = jnp.where(other > my, 0, 1)
        return pltpu.make_async_remote_copy(
            src_ref=sloc.at[which], dst_ref=crecv.at[my], send_sem=cs.at[k], recv_sem=cr.at[k],
            device_id=(me, other), device_id_type=MESH)

    def d_copy(k):
        return pltpu.make_async_remote_copy(
            src_ref=decs, dst_ref=decr.at[my], send_sem=es.at[k], recv_sem=er.at[k],
            device_id=(me, mate(k)), device_id_type=MESH)

    def p_copy(k):
        return pltpu.make_async_remote_copy(
            src_ref=pst.at[mate(k)], dst_ref=precv.at[my], send_sem=ps.at[k], recv_sem=pr.at[k],
            device_id=(me, mate(k)), device_id_type=MESH)

    def each(n, act):
        def step(k, carry):
            act(k)
            return carry

        lax.fori_loop(1, n, step, 0)

    def spread_near(slot, send, recv, ka):
        each(n_b, lambda kb: near(slot, send, recv, ka, kb).start())

    def first(slot, send, recv, fsend, frecv):
        each(n_a, lambda ka: far(slot, send, recv, ka).start())
        spread_near(slot, fsend, frecv, 0)

    def pass_on(slot, send, recv, fsend, frecv):
        def one(ka):
            far(slot, send, recv, ka).wait_recv()
            spread_near(slot, fsend, frecv, ka)

        each(n_a, one)

    def arrive(slot, fsend, frecv, ka):
        each(n_b, lambda kb: near(slot, fsend, frecv, ka, kb).wait_recv())

    def settle(slot, send, recv, fsend, frecv):
        each(n_a, lambda ka: far(slot, send, recv, ka).wait_send())

        def one(ka, carry):
            each(n_b, lambda kb: near(slot, fsend, frecv, ka, kb).wait_send())
            return carry

        lax.fori_loop(0, n_a, one, 0)

    inner = x.shape[1]
    wcols = w.shape[0]
    if halved:
        wall[my, :, pl.ds(pl.multiple_of(me * half, LANES), half)] = w[:, pl.ds(pl.multiple_of(my * half, LANES), half)]
    elif wide:
        wall[:, pl.ds(pl.multiple_of(me * rows, LANES), rows)] = w[...]
    else:
        wall[me] = w[...]
    first(w_slot, wzs, wzr, wfs, wfr)
    loads[0].wait()
    loads[1].wait()
    loads[2].wait()
    pass_on(w_slot, wzs, wzr, wfs, wfr)
    each(n_dp, lambda k: a_copy(k).start())
    if wide:
        trecv[blk(me), :] = tok[:, pl.ds(pl.multiple_of(me * rows, LANES), rows)]
    else:
        trecv[blk(me), :] = tok[me]
    proj[...] = jnp.zeros_like(proj)
    qacc[...] = jnp.zeros_like(qacc)
    ds[...] = jnp.zeros_like(ds)
    rowt[...] = jnp.zeros_like(rowt)
    spread_m[...] = jnp.where(iota((LANES, inner), 0) == iota((LANES, inner), 1) // width, 1.0, 0.0).astype(BF16)
    gather_m[...] = jnp.where(iota((inner, LANES), 1) == iota((inner, LANES), 0) // width, 1.0, 0.0).astype(BF16)
    head = iota((t, LANES), 1) // width

    def outer(q, carry):
        x4 = x[:, lanes(q)]
        zero = jnp.zeros_like(x4)
        xm = jnp.concatenate([jnp.where(head == j, x4, zero) for j in range(gh)], axis=0)
        dall[q] = dot_nt(xm, g[:, lanes(q)])
        return carry

    lax.fori_loop(0, groups, outer, 0)

    def land(ka, carry):
        arrive(w_slot, wfs, wfr, ka)
        if halved:
            across(ka).start()
        return carry

    lax.fori_loop(0, n_a, land, 0)
    if halved:
        lax.fori_loop(0, n_a, lambda ka, carry: (across(ka).wait_recv(), carry)[1], 0)
        total = None
        for k in range(n_ctx):
            picked = jnp.concatenate(
                [tok[:, i * rows + k * half:i * rows + (k + 1) * half] for i in range(n_dp)], axis=1)
            term = dot_nt(picked, wall[k])
            total = term if total is None else total + term
        proj[:, :wcols] = total
    elif wide:
        proj[:, :wcols] = dot_nt(tok[...], wall[...])
    else:
        def shard(i, carry):
            proj[:, :wcols] += dot_nt(tok[i], wall[i])
            return carry

        lax.fori_loop(0, n_dp, shard, 0)
    rate_scale = -jnp.exp(vec[0:1, :])
    b = proj[:, :STATE].astype(BF16)
    z = proj[:, STATE:STATE + LANES] + vec[1:2, :]
    dt = jnp.maximum(z, 0.0) + jnp.log1p(jnp.exp(-jnp.abs(z)))
    row_i, col_i = iota((t, t), 0), iota((t, t), 1)
    lower = jnp.where(row_i >= col_i, 1.0, 0.0).astype(BF16)
    upper = jnp.where(col_i >= row_i, 1.0, 0.0).astype(BF16)
    cum = dot_exact(lower, rate_scale * dt)
    cum_r[...] = cum
    dt_r[...] = dt
    cumt[...] = cum.T
    last = cum_r[t - 1:t, :]
    to_end = jnp.exp(last - cum)
    wgt = to_end * dt
    grow = jnp.exp(cum)
    w_bf = wgt.astype(BF16)
    e_bf = grow.astype(BF16)
    cv = c[...]
    bt = b.astype(F32).T.astype(BF16)
    ct = cv.astype(F32).T.astype(BF16)

    span = [slice(q * LANES, (q + 1) * LANES) for q in range(groups)]
    for at in span:
        xw[:, at] = (dot(w_bf, spread_m[:, at]) * x[:, at].astype(F32)).astype(BF16)
        gwt[:, at] = (dot(e_bf, spread_m[:, at]) * g[:, at].astype(F32)).astype(BF16)
    sloc[0] = dot(bt, xw[...]).astype(BF16)
    sloc[1] = dot(ct, gwt[...]).astype(BF16)
    each(n_ctx, lambda k: c_copy(k).start())
    if n_ctx > 2:
        decs[...] = jnp.broadcast_to(jnp.exp(last), decs.shape)
        crecv[my] = jnp.zeros(crecv.shape[1:], BF16)
        decr[my] = jnp.zeros(decr.shape[1:], F32)
        each(n_ctx, lambda k: d_copy(k).start())

    scores = dot_nt(b, cv)
    causal = col_i >= row_i

    def mix(q, carry):
        g4 = g[:, lanes(q)]
        shift = lax.rem(LANES - gh * q, LANES)
        cum_s = pltpu.roll(cum_r[...], shift, 1)
        dt_s = pltpu.roll(dt_r[...], shift, 1)
        total = ds[...]
        quot = qacc[...]
        mixed = []
        for j in range(gh):
            h = gh * q + j
            spread = cumt[pl.ds(h, 1), :] - cum_s[:, j:j + 1]
            factor = jnp.exp(jnp.where(causal, spread, -1e30))
            step = dt_s[:, j:j + 1]
            d = dall[q, j * t:(j + 1) * t]
            fs = factor * scores
            mixed.append((fs * step).astype(BF16))
            u = d * fs
            quot = jnp.where(col_i == h, jnp.sum(u, axis=1, keepdims=True), quot)
            rowt[pl.ds(h, 1), :] = jnp.sum(u * step, axis=0, keepdims=True)
            total = total + d * (factor * step)
        ds[...] = total
        qacc[...] = quot
        out = dot(jnp.concatenate(mixed, axis=0), g4)
        acc = dexp[:, lanes(q)] * g4.astype(F32)
        for j in range(gh):
            acc = acc + jnp.where(head == j, out[j * t:(j + 1) * t], 0.0)
        dx[:, lanes(q)] = acc
        return carry

    lax.fori_loop(0, groups, mix, 0)
    each(n_ctx, lambda k: c_copy(k).wait_recv())
    if n_ctx > 2:
        each(n_ctx, lambda k: d_copy(k).wait_recv())

    sv = sg = jnp.zeros((t, LANES), F32)
    db2 = dc2 = jnp.zeros((t, STATE), F32)
    gs = jnp.zeros((8, LANES), F32)
    for at in span:
        e, et = spread_m[:, at], gather_m[at, :]
        if n_ctx == 2:
            got = crecv[1 - my, :, at]
            none = jnp.zeros_like(got)
            s4 = jnp.where(my > 0, got, none)
            g4s = jnp.where(my < 1, got, none)
        else:
            s = jnp.zeros((STATE, LANES), F32)
            k = s
            for i in range(n_ctx):
                dec = dot_split(decr[i], e)[0:1]
                s = jnp.where(i < my, dec * s + crecv[i, :, at].astype(F32), s)
            for i in reversed(range(n_ctx)):
                dec = dot_split(decr[i], e)[0:1]
                k = jnp.where(i > my, dec * k + crecv[i, :, at].astype(F32), k)
            s4, g4s = s.astype(BF16), k.astype(BF16)
            both = jnp.sum(s * k, axis=0, keepdims=True)
            gs = gs + dot_split(jnp.broadcast_to(both, (8, LANES)), et)
        us = dot(cv, s4)
        ug = dot(b, g4s)
        sv = sv + dot_split(x[:, at].astype(F32) * ug, et)
        sg = sg + dot_split(g[:, at].astype(F32) * us, et)
        db2 = db2 + dot_nt(xw[:, at], g4s)
        dc2 = dc2 + dot_nt(gwt[:, at], s4)
        gx[:, at] = (dx[:, at] + dot(w_bf, e) * ug).astype(BF16)
    dsv = ds[...]
    db = dot_split(dsv, cv) + db2
    dc = dot_split(dsv.T, b) + dc2
    gc[...] = dc.astype(BF16)
    quot = qacc[...]
    v = sv
    vw = v * wgt
    dcum = rowt[...].T + grow * sg - dt * quot - vw
    tail = jnp.sum(vw, axis=0, keepdims=True)
    if n_ctx > 2:
        tail = tail + jnp.exp(last) * gs[0:1, :]
    dcum = dcum + jnp.where(row_i == t - 1, tail, 0.0)
    drate = dot_exact(upper, dcum)
    ddt = quot + v * to_end + rate_scale * drate
    dz = ddt / (1.0 + jnp.exp(-z))
    proj[...] = jnp.zeros_like(proj)
    proj[:, :STATE] = db.astype(BF16).astype(F32)
    proj[:, STATE:cols] = dz[:, :heads]
    whole = proj[...]
    gall[:, blk(me)] = whole.T[:wcols].astype(BF16)
    first(g_slot, gzs, gzr, gfs, gfr)
    gp[...] = whole[:, :cols].astype(BF16)
    pass_on(g_slot, gzs, gzr, gfs, gfr)
    each(n_dp, lambda k: a_copy(k).wait_recv())
    lax.fori_loop(0, n_a, lambda ka, carry: (arrive(g_slot, gfs, gfr, ka), carry)[1], 0)
    part[...] = dot(gall[...], trecv[...])
    for o in range(n_ctx):
        pst[o] = part[o * cb:o * cb + cbp, :]
    each(n_ctx, lambda k: p_copy(k).start())
    each(n_ctx, lambda k: p_copy(k).wait_recv())

    def add(k, acc):
        return acc + precv[mate(k)]

    total = lax.fori_loop(1, n_ctx, add, pst[my])
    gw[...] = (total * (1.0 / n_dp)).T[:, :cb]
    settle(w_slot, wzs, wzr, wfs, wfr)
    if halved:
        lax.fori_loop(0, n_a, lambda ka, carry: (across(ka).wait_send(), carry)[1], 0)
    each(n_dp, lambda k: a_copy(k).wait_send())
    settle(g_slot, gzs, gzr, gfs, gfr)
    each(n_ctx, lambda k: c_copy(k).wait_send())
    each(n_ctx, lambda k: p_copy(k).wait_send())
    if n_ctx > 2:
        each(n_ctx, lambda k: d_copy(k).wait_send())


def store(*refs):
    sems = refs[-1]
    copies = [pltpu.make_async_copy(refs[i], refs[4 + i], sems.at[i]) for i in range(4)]
    for copy in copies:
        copy.start()
    for copy in copies:
        copy.wait()


def per_device(layer_in, inner_act, readout, w_in, a_log, dt_bias, d_skip, grad_out):
    n_dp, n_ctx = lax.axis_size("dp"), lax.axis_size("ctx")
    tokens, x, c, g = layer_in[0], inner_act[0], readout[0], grad_out[0]
    t, inner = x.shape
    rows, cols = w_in.shape
    heads = a_log.shape[0]
    width = inner // heads
    wcols = up(cols, 16)
    wide = rows % LANES == 0
    wt = jnp.pad(w_in.T, ((0, wcols - cols), (0, 0)))
    if not wide:
        tokens = jnp.swapaxes(tokens.reshape(t, n_dp, rows), 0, 1)
    vec = jnp.pad(jnp.stack([a_log, dt_bias]), ((0, 6), (0, LANES - heads)))
    dexp = jnp.repeat(d_skip, width)[None]
    cb = cols // n_ctx
    cbp = up(cb, 8)
    vm = pltpu.VMEM
    n_a = n_dp // inner_group(n_dp)
    if not wide:
        wall = (n_dp, wcols, rows)
    elif rows % (n_ctx * LANES) == 0 and n_ctx == 2:
        wall = (n_ctx, wcols, n_dp * rows // n_ctx)
    else:
        wall = (wcols, n_dp * rows)
    scratch = [
        vm(tokens.shape, BF16),
        vm((t, inner), BF16),
        vm((t, inner), BF16),
        vm(wall, BF16),
        vm((n_dp * t, rows), BF16),
        vm((wcols, n_dp * t), BF16),
        vm((2, STATE, inner), BF16),
        vm((n_ctx, STATE, inner), BF16),
        vm((inner // LANES, LANES // width * t, t), F32),
        vm((LANES, inner), BF16),
        vm((inner, LANES), BF16),
        vm((t, inner), BF16),
        vm((t, inner), BF16),
        vm((t, inner), F32),
        vm((t, 2 * LANES), F32),
        vm((t, LANES), F32),
        vm((t, LANES), F32),
        vm((LANES, t), F32),
        vm((LANES, t), F32),
        vm((t, LANES), F32),
        vm((t, t), F32),
        vm((wcols, rows), F32),
        vm((n_ctx, cbp, rows), F32),
        vm((n_ctx, cbp, rows), F32),
        vm((8, LANES), F32),
        vm((n_ctx, 8, LANES), F32),
    ]
    dma = pltpu.SemaphoreType.DMA
    scratch += [dma((n_a,))] * 2 + [dma((n_dp,))] * 4 + [dma((n_a,))] * 2 + [dma((n_dp,))] * 2
    scratch += [dma((n_ctx,))] * 6 + [dma((n_a,))] * 2 + [dma((3,))]
    hbm = pl.BlockSpec(memory_space=pltpu.HBM)
    spec = pl.BlockSpec(memory_space=pltpu.VMEM)
    cfg = (n_dp, n_ctx, t, rows, heads, width, cols)
    results = pl.pallas_call(
        functools.partial(kernel, cfg),
        out_shape=(
            jax.ShapeDtypeStruct((t, inner), BF16),
            jax.ShapeDtypeStruct((t, STATE), BF16),
            jax.ShapeDtypeStruct((t, cols), BF16),
            jax.ShapeDtypeStruct((rows, cb), F32),
        ),
        in_specs=[hbm] * 3 + [spec] * 4,
        out_specs=(spec,) * 4,
        scratch_shapes=scratch,
        compiler_params=pltpu.CompilerParams(
            collective_id=0, has_side_effects=True, vmem_limit_bytes=48 * 1024 * 1024),
        name="ssm_backward",
    )(tokens, x, g, c, wt, vec, dexp)
    gx, gc, gp, gw = pl.pallas_call(
        store,
        out_shape=tuple(jax.ShapeDtypeStruct(r.shape, r.dtype) for r in results),
        in_specs=[spec] * 4,
        out_specs=(hbm,) * 4,
        scratch_shapes=[dma((4,))],
        name="store_results",
    )(*results)
    return (gx[None], gc[None], gp[None], gw)


def solution(mesh):
    in_specs = (
        P("dp", "ctx", None),
        P("dp", "ctx", None),
        P("dp", "ctx", None),
        P("dp", None),
        P(),
        P(),
        P(),
        P("dp", "ctx", None),
    )
    out_specs = (P("dp", "ctx", None), P("dp", "ctx", None), P("dp", "ctx", None), P("dp", "ctx"))
    return jax.shard_map(
        per_device, mesh=mesh, in_specs=in_specs, out_specs=out_specs, check_vma=False
    )
```

```python
import functools

import jax
import jax.numpy as jnp
from jax import lax
from jax.experimental import pallas as pl
from jax.experimental.pallas import tpu as pltpu
from jax.sharding import PartitionSpec as P

STATE = 64
LANES = 128
MESH = pl.DeviceIdType.MESH
F32 = jnp.float32
BF16 = jnp.bfloat16


def inner_group(n):
    b = 1
    while b * b < n and n % (2 * b) == 0:
        b *= 2
    return b


def up(n, m):
    return -(-n // m) * m


def dot(a, b):
    return jnp.dot(a, b, preferred_element_type=F32)


def dot_nt(a, b):
    return lax.dot_general(a, b, (((1,), (1,)), ((), ())), preferred_element_type=F32)


def split(v):
    hi = v.astype(BF16)
    return hi, (v - hi.astype(F32)).astype(BF16)


def dot_split(v, b):
    hi, lo = split(v)
    return dot(hi, b) + dot(lo, b)


def dot_exact(sel, v):
    hi, rest = v.astype(BF16), None
    rest = v - hi.astype(F32)
    mid, low = split(rest)
    return dot(sel, hi) + dot(sel, mid) + dot(sel, low)


def iota(shape, dim):
    return lax.broadcasted_iota(jnp.int32, shape, dim)


def kernel(cfg, tok_h, x_h, g_h, c, w_own, a_log, dt_bias, d_skip, gx_h, gc_h, gp_h, gw_h, gx, gc, gp, gw, w, vec, tok, x, g, wall, trecv, gall, sloc, crecv,
           dall, spread_m, gather_m, xw, gwt, dx, proj, cum_r, dt_r, cumt, rowt, qacc, ds, part, pst, precv, zst, zrecv,
           decs, decr, wzs, wzr, wfs, wfr, as_, ar, gzs, gzr, gfs, gfr, os, cs, cr, ps, pr, es, er, ms, mr, ls):
    n_dp, n_ctx, t, rows, heads, width, cols = cfg
    wide = rows % LANES == 0
    unroll = True
    halved = wide and rows % (n_ctx * LANES) == 0 and n_ctx == 2
    half = rows // n_ctx
    n_b = inner_group(n_dp)
    n_a = n_dp // n_b
    my_a, my_b = lax.div(lax.axis_index("dp"), n_b), lax.rem(lax.axis_index("dp"), n_b)
    loads = [pltpu.make_async_copy(src, dst, ls.at[i]) for i, (src, dst) in enumerate(((x_h, x), (g_h, g), (tok_h, tok)))]
    for load in loads:
        load.start()
    groups = x.shape[1] // LANES
    gh = LANES // width
    cb = cols // n_ctx
    cbp = up(cb, 16)
    me = lax.axis_index("dp")
    my = lax.axis_index("ctx")

    def peer(k):
        return lax.rem(me + k, n_dp)

    def mate(k):
        return lax.rem(my + k, n_ctx)

    def col(ref, i):
        return ref.at[:, pl.ds(pl.multiple_of(i * rows, LANES), rows)] if wide else ref.at[i]

    def blk(i):
        return pl.ds(pl.multiple_of(i * t, LANES), t)

    def lanes(q):
        return pl.ds(pl.multiple_of(q * LANES, LANES), LANES)

    barrier = pltpu.get_barrier_semaphore()

    def greet(k, carry):
        pl.semaphore_signal(barrier, inc=1, device_id=(peer(k), my), device_id_type=MESH)
        return carry

    def greet_mate(k, carry):
        pl.semaphore_signal(barrier, inc=1, device_id=(me, mate(k)), device_id_type=MESH)
        return carry

    lax.fori_loop(1, n_dp, greet, 0)
    lax.fori_loop(1, n_ctx, greet_mate, 0)
    pl.semaphore_wait(barrier, n_dp + n_ctx - 2)

    def origin(ka, kb):
        return lax.rem(my_a + n_a - ka, n_a) * n_b + lax.rem(my_b + n_b - kb, n_b)

    def w_slot(i):
        if halved:
            return wall.at[my, :, pl.ds(pl.multiple_of(i * half, LANES), half)]
        return col(wall, i)

    def g_slot(i):
        return gall.at[:, blk(lax.rem(i, n_b))]

    def far(slot, send, recv, ka):
        return pltpu.make_async_remote_copy(
            src_ref=slot(me), dst_ref=slot(me), send_sem=send.at[ka], recv_sem=recv.at[ka],
            device_id=(lax.rem(my_a + ka, n_a) * n_b + my_b, my), device_id_type=MESH)

    def near(slot, send, recv, ka, kb):
        i = origin(ka, 0)
        return pltpu.make_async_remote_copy(
            src_ref=slot(i), dst_ref=slot(i), send_sem=send.at[ka * n_b + kb], recv_sem=recv.at[ka * n_b + kb],
            device_id=(my_a * n_b + lax.rem(my_b + kb, n_b), my), device_id_type=MESH)

    def across(ka):
        i = lax.rem(my_a + n_a - ka, n_a) * n_b
        block = wall.at[my, :, pl.ds(pl.multiple_of(i * half, LANES), n_b * half)]
        return pltpu.make_async_remote_copy(
            src_ref=block, dst_ref=block, send_sem=ms.at[ka], recv_sem=mr.at[ka],
            device_id=(me, 1 - my), device_id_type=MESH)

    def a_copy(kb, a):
        b_to = lax.rem(my_b + kb, n_b)
        return pltpu.make_async_remote_copy(
            src_ref=col(tok, a * n_b + b_to), dst_ref=trecv.at[a, blk(my_b), :],
            send_sem=as_.at[kb * n_a + a], recv_sem=ar.at[kb * n_a + a],
            device_id=(my_a * n_b + b_to, my), device_id_type=MESH)

    def a_each(act):
        def one(a, carry):
            each(n_b, lambda kb: act(a_copy(kb, a)))
            return carry

        lax.fori_loop(0, n_a, one, 0)

    def z_copy(k):
        a_to = lax.rem(my_a + k, n_a)
        return pltpu.make_async_remote_copy(
            src_ref=zst.at[a_to], dst_ref=zrecv.at[my_a], send_sem=gzs.at[k], recv_sem=gzr.at[k],
            device_id=(a_to * n_b + my_b, my), device_id_type=MESH)

    def c_copy(k):
        other = mate(k)
        which = jnp.where(other > my, 0, 1)
        return pltpu.make_async_remote_copy(
            src_ref=sloc.at[which], dst_ref=crecv.at[my], send_sem=cs.at[k], recv_sem=cr.at[k],
            device_id=(me, other), device_id_type=MESH)

    def d_copy(k):
        return pltpu.make_async_remote_copy(
            src_ref=decs, dst_ref=decr.at[my], send_sem=es.at[k], recv_sem=er.at[k],
            device_id=(me, mate(k)), device_id_type=MESH)

    def p_copy(k):
        return pltpu.make_async_remote_copy(
            src_ref=pst.at[mate(k)], dst_ref=precv.at[my], send_sem=ps.at[k], recv_sem=pr.at[k],
            device_id=(me, mate(k)), device_id_type=MESH)

    def each(n, act):
        def step(k, carry):
            act(k)
            return carry

        lax.fori_loop(1, n, step, 0)

    def spread_near(slot, send, recv, ka):
        each(n_b, lambda kb: near(slot, send, recv, ka, kb).start())

    def first(slot, send, recv, fsend, frecv):
        each(n_a, lambda ka: far(slot, send, recv, ka).start())
        spread_near(slot, fsend, frecv, 0)

    def pass_on(slot, send, recv, fsend, frecv):
        def one(ka):
            far(slot, send, recv, ka).wait_recv()
            spread_near(slot, fsend, frecv, ka)

        each(n_a, one)

    def arrive(slot, fsend, frecv, ka):
        each(n_b, lambda kb: near(slot, fsend, frecv, ka, kb).wait_recv())

    def settle(slot, send, recv, fsend, frecv):
        each(n_a, lambda ka: far(slot, send, recv, ka).wait_send())

        def one(ka, carry):
            each(n_b, lambda kb: near(slot, fsend, frecv, ka, kb).wait_send())
            return carry

        lax.fori_loop(0, n_a, one, 0)

    inner = x.shape[1]
    wcols = w.shape[0]
    w[...] = jnp.zeros_like(w)
    w[:cols, :] = w_own[...]
    if halved:
        wall[my, :, pl.ds(pl.multiple_of(me * half, LANES), half)] = w[:, pl.ds(pl.multiple_of(my * half, LANES), half)]
    elif wide:
        wall[:, pl.ds(pl.multiple_of(me * rows, LANES), rows)] = w[...]
    else:
        wall[me] = w[...]
    first(w_slot, wzs, wzr, wfs, wfr)
    vec[...] = jnp.zeros_like(vec)
    for i, ref in enumerate((a_log, dt_bias, d_skip)):
        vec[i:i + 1, :heads] = ref[...]
    for load in loads:
        load.wait()
    pass_on(w_slot, wzs, wzr, wfs, wfr)
    a_each(lambda copy: copy.start())
    for a in range(n_a):
        trecv[a, blk(my_b), :] = col(tok, a * n_b + my_b)[...]
    proj[...] = jnp.zeros_like(proj)
    qacc[...] = jnp.zeros_like(qacc)
    ds[...] = jnp.zeros_like(ds)
    rowt[...] = jnp.zeros_like(rowt)
    spread_m[...] = jnp.where(iota((LANES, inner), 0) == iota((LANES, inner), 1) // width, 1.0, 0.0).astype(BF16)
    gather_m[...] = jnp.where(iota((inner, LANES), 1) == iota((inner, LANES), 0) // width, 1.0, 0.0).astype(BF16)
    head = iota((t, LANES), 1) // width

    def outer(q, carry):
        x4 = x[:, lanes(q)]
        zero = jnp.zeros_like(x4)
        xm = jnp.concatenate([jnp.where(head == j, x4, zero) for j in range(gh)], axis=0)
        dall[q] = dot_nt(xm, g[:, lanes(q)])
        return carry

    lax.fori_loop(0, groups, outer, 0)

    def land(ka, carry):
        arrive(w_slot, wfs, wfr, ka)
        if halved:
            across(ka).start()
        return carry

    lax.fori_loop(0, n_a, land, 0)
    if halved:
        lax.fori_loop(0, n_a, lambda ka, carry: (across(ka).wait_recv(), carry)[1], 0)
        total = None
        for k in range(n_ctx):
            picked = jnp.concatenate(
                [tok[:, i * rows + k * half:i * rows + (k + 1) * half] for i in range(n_dp)], axis=1)
            term = dot_nt(picked, wall[k])
            total = term if total is None else total + term
        proj[:, :wcols] = total
    elif wide:
        proj[:, :wcols] = dot_nt(tok[...], wall[...])
    else:
        def shard(i, carry):
            proj[:, :wcols] += dot_nt(tok[i], wall[i])
            return carry

        lax.fori_loop(0, n_dp, shard, 0)
    rate_scale = -jnp.exp(vec[0:1, :])
    b = proj[:, :STATE].astype(BF16)
    z = proj[:, STATE:STATE + LANES] + vec[1:2, :]
    dt = jnp.maximum(z, 0.0) + jnp.log1p(jnp.exp(-jnp.abs(z)))
    row_i, col_i = iota((t, t), 0), iota((t, t), 1)
    lower = jnp.where(row_i >= col_i, 1.0, 0.0).astype(BF16)
    upper = jnp.where(col_i >= row_i, 1.0, 0.0).astype(BF16)
    cum = dot_exact(lower, rate_scale * dt)
    cum_r[...] = cum
    dt_r[...] = dt
    cumt[...] = cum.T
    last = cum_r[t - 1:t, :]
    to_end = jnp.exp(last - cum)
    wgt = to_end * dt
    grow = jnp.exp(cum)
    w_bf = wgt.astype(BF16)
    e_bf = grow.astype(BF16)
    ct = c[...]
    bt = b.astype(F32).T.astype(BF16)
    cv = ct.astype(F32).T.astype(BF16)
    skip_hi, skip_lo = split(vec[...])

    span = [slice(q * LANES, (q + 1) * LANES) for q in range(groups)]
    for at in span:
        xw[:, at] = (dot(w_bf, spread_m[:, at]) * x[:, at].astype(F32)).astype(BF16)
        gwt[:, at] = (dot(e_bf, spread_m[:, at]) * g[:, at].astype(F32)).astype(BF16)
    sloc[0] = dot(bt, xw[...]).astype(BF16)
    sloc[1] = dot(ct, gwt[...]).astype(BF16)
    each(n_ctx, lambda k: c_copy(k).start())
    if n_ctx > 2:
        decs[...] = jnp.broadcast_to(jnp.exp(last), decs.shape)
        crecv[my] = jnp.zeros(crecv.shape[1:], BF16)
        decr[my] = jnp.zeros(decr.shape[1:], F32)
        each(n_ctx, lambda k: d_copy(k).start())

    scores = dot_nt(b, cv)
    causal = col_i >= row_i

    def mix(q, carry):
        g4 = g[:, lanes(q)]
        shift = lax.rem(LANES - gh * q, LANES)
        cum_s = pltpu.roll(cum_r[...], shift, 1)
        dt_s = pltpu.roll(dt_r[...], shift, 1)
        total = ds[...]
        quot = qacc[...]
        mixed = []
        for j in range(gh):
            h = gh * q + j
            spread = cumt[pl.ds(h, 1), :] - cum_s[:, j:j + 1]
            factor = jnp.exp(jnp.where(causal, spread, -1e30))
            step = dt_s[:, j:j + 1]
            d = dall[q, j * t:(j + 1) * t]
            fs = factor * scores
            mixed.append((fs * step).astype(BF16))
            u = d * fs
            quot = jnp.where(col_i == h, jnp.sum(u, axis=1, keepdims=True), quot)
            rowt[pl.ds(h, 1), :] = jnp.sum(u * step, axis=0, keepdims=True)
            total = total + d * (factor * step)
        ds[...] = total
        qacc[...] = quot
        out = dot(jnp.concatenate(mixed, axis=0), g4)
        skip = dot(skip_hi, spread_m[:, lanes(q)]) + dot(skip_lo, spread_m[:, lanes(q)])
        acc = skip[2:3] * g4.astype(F32)
        for j in range(gh):
            acc = acc + jnp.where(head == j, out[j * t:(j + 1) * t], 0.0)
        dx[:, lanes(q)] = acc
        return carry

    lax.fori_loop(0, groups, mix, 0, unroll=unroll)
    each(n_ctx, lambda k: c_copy(k).wait_recv())
    if n_ctx > 2:
        each(n_ctx, lambda k: d_copy(k).wait_recv())

    sv = sg = jnp.zeros((t, LANES), F32)
    db2 = dc2 = jnp.zeros((t, STATE), F32)
    gs = jnp.zeros((8, LANES), F32)
    for at in span:
        e, et = spread_m[:, at], gather_m[at, :]
        if n_ctx == 2:
            got = crecv[1 - my, :, at]
            none = jnp.zeros_like(got)
            s4 = jnp.where(my > 0, got, none)
            g4s = jnp.where(my < 1, got, none)
        else:
            s = jnp.zeros((STATE, LANES), F32)
            k = s
            for i in range(n_ctx):
                dec = dot_split(decr[i], e)[0:1]
                s = jnp.where(i < my, dec * s + crecv[i, :, at].astype(F32), s)
            for i in reversed(range(n_ctx)):
                dec = dot_split(decr[i], e)[0:1]
                k = jnp.where(i > my, dec * k + crecv[i, :, at].astype(F32), k)
            s4, g4s = s.astype(BF16), k.astype(BF16)
            both = jnp.sum(s * k, axis=0, keepdims=True)
            gs = gs + dot_split(jnp.broadcast_to(both, (8, LANES)), et)
        us = dot(cv, s4)
        ug = dot(b, g4s)
        sv = sv + dot_split(x[:, at].astype(F32) * ug, et)
        sg = sg + dot_split(g[:, at].astype(F32) * us, et)
        db2 = db2 + dot_nt(xw[:, at], g4s)
        dc2 = dc2 + dot_nt(gwt[:, at], s4)
        gx[:, at] = (dx[:, at] + dot(w_bf, e) * ug).astype(BF16)
    stores = [pltpu.make_async_copy(src, dst, os.at[i]) for i, (src, dst) in enumerate(
        ((gx, gx_h), (gc, gc_h), (gp, gp_h), (gw, gw_h)))]
    stores[0].start()
    dsv = ds[...]
    db = dot_split(dsv, cv) + db2
    dc = dot_split(dsv.T, b) + dc2
    gc[...] = dc.T.astype(BF16)
    stores[1].start()
    quot = qacc[...]
    v = sv
    vw = v * wgt
    dcum = rowt[...].T + grow * sg - dt * quot - vw
    tail = jnp.sum(vw, axis=0, keepdims=True)
    if n_ctx > 2:
        tail = tail + jnp.exp(last) * gs[0:1, :]
    dcum = dcum + jnp.where(row_i == t - 1, tail, 0.0)
    drate = dot_exact(upper, dcum)
    ddt = quot + v * to_end + rate_scale * drate
    dz = ddt / (1.0 + jnp.exp(-z))
    proj[...] = jnp.zeros_like(proj)
    proj[:, :STATE] = db.astype(BF16).astype(F32)
    proj[:, STATE:cols] = dz[:, :heads]
    whole = proj[...]
    turned = whole.T[:wcols].astype(BF16)
    gall[:, blk(my_b)] = turned
    spread_near(g_slot, gfs, gfr, 0)
    gp[...] = turned[:cols]
    stores[2].start()
    part[...] = jnp.zeros_like(part)
    a_each(lambda copy: copy.wait_recv())
    arrive(g_slot, gfs, gfr, 0)
    for a in range(n_a):
        part[a, :wcols] = dot(gall[...], trecv[a])
        for o in range(n_ctx):
            pst[o, a] = part[a, o * cb:o * cb + cbp, :].astype(BF16)
    each(n_ctx, lambda k: p_copy(k).start())
    each(n_ctx, lambda k: p_copy(k).wait_recv())

    for a in range(n_a):
        zst[a] = lax.fori_loop(
            1, n_ctx, lambda k, acc: acc + precv[mate(k), a].astype(F32), pst[my, a].astype(F32)).astype(BF16)
    each(n_a, lambda k: z_copy(k).start())
    each(n_a, lambda k: z_copy(k).wait_recv())
    total = lax.fori_loop(
        1, n_a, lambda k, acc: acc + zrecv[lax.rem(my_a + k, n_a)].astype(F32), zst[my_a].astype(F32))
    gw[...] = (total * (1.0 / n_dp))[:cb]
    stores[3].start()
    settle(w_slot, wzs, wzr, wfs, wfr)
    if halved:
        lax.fori_loop(0, n_a, lambda ka, carry: (across(ka).wait_send(), carry)[1], 0)
    a_each(lambda copy: copy.wait_send())
    each(n_b, lambda kb: near(g_slot, gfs, gfr, 0, kb).wait_send())
    each(n_a, lambda k: z_copy(k).wait_send())
    for copy in stores:
        copy.wait()
    each(n_ctx, lambda k: c_copy(k).wait_send())
    each(n_ctx, lambda k: p_copy(k).wait_send())
    if n_ctx > 2:
        each(n_ctx, lambda k: d_copy(k).wait_send())


def store(*refs):
    sems = refs[-1]
    copies = [pltpu.make_async_copy(refs[i], refs[4 + i], sems.at[i]) for i in range(4)]
    for copy in copies:
        copy.start()
    for copy in copies:
        copy.wait()


def per_device(layer_in, inner_act, readout, w_in, a_log, dt_bias, d_skip, grad_out):
    n_dp, n_ctx = lax.axis_size("dp"), lax.axis_size("ctx")
    tokens, x, c, g = layer_in[0], inner_act[0], readout[0], grad_out[0]
    t, inner = x.shape
    rows, cols = w_in.shape
    heads = a_log.shape[0]
    width = inner // heads
    wcols = up(cols, 16)
    wide = rows % LANES == 0
    wt = w_in.T
    if not wide:
        tokens = jnp.swapaxes(tokens.reshape(t, n_dp, rows), 0, 1)
    cb = cols // n_ctx
    cbp = up(cb, 16)
    part_rows = up(max(wcols, cols - cb + cbp), 8)
    vm = pltpu.VMEM
    n_a = n_dp // inner_group(n_dp)
    if not wide:
        wall = (n_dp, wcols, rows)
    elif rows % (n_ctx * LANES) == 0 and n_ctx == 2:
        wall = (n_ctx, wcols, n_dp * rows // n_ctx)
    else:
        wall = (wcols, n_dp * rows)
    shapes = (
        jax.ShapeDtypeStruct((t, inner), BF16),
        jax.ShapeDtypeStruct((STATE, t), BF16),
        jax.ShapeDtypeStruct((cols, t), BF16),
        jax.ShapeDtypeStruct((cb, rows), F32),
    )
    n_b = inner_group(n_dp)
    scratch = [vm(r.shape, r.dtype) for r in shapes] + [
        vm((wcols, rows), BF16),
        vm((8, LANES), F32),
        vm(tokens.shape, BF16),
        vm((t, inner), BF16),
        vm((t, inner), BF16),
        vm(wall, BF16),
        vm((n_a, n_b * t, rows), BF16),
        vm((wcols, n_b * t), BF16),
        vm((2, STATE, inner), BF16),
        vm((n_ctx, STATE, inner), BF16),
        vm((inner // LANES, LANES // width * t, t), F32),
        vm((LANES, inner), BF16),
        vm((inner, LANES), BF16),
        vm((t, inner), BF16),
        vm((t, inner), BF16),
        vm((t, inner), F32),
        vm((t, 2 * LANES), F32),
        vm((t, LANES), F32),
        vm((t, LANES), F32),
        vm((LANES, t), F32),
        vm((LANES, t), F32),
        vm((t, LANES), F32),
        vm((t, t), F32),
        vm((n_a, part_rows, rows), F32),
        vm((n_ctx, n_a, cbp, rows), BF16),
        vm((n_ctx, n_a, cbp, rows), BF16),
        vm((n_a, cbp, rows), BF16),
        vm((n_a, cbp, rows), BF16),
        vm((8, LANES), F32),
        vm((n_ctx, 8, LANES), F32),
    ]
    dma = pltpu.SemaphoreType.DMA
    scratch += [dma((n_a,))] * 2 + [dma((n_dp,))] * 4 + [dma((n_a,))] * 2 + [dma((n_dp,))] * 2 + [dma((4,))]
    scratch += [dma((n_ctx,))] * 6 + [dma((n_a,))] * 2 + [dma((3,))]
    hbm = pl.BlockSpec(memory_space=pltpu.HBM)
    spec = pl.BlockSpec(memory_space=pltpu.VMEM)
    cfg = (n_dp, n_ctx, t, rows, heads, width, cols)
    results = pl.pallas_call(
        functools.partial(kernel, cfg),
        out_shape=shapes,
        in_specs=[hbm] * 3 + [spec] * 5,
        out_specs=(hbm,) * 4,
        scratch_shapes=scratch,
        compiler_params=pltpu.CompilerParams(
            collective_id=0, has_side_effects=True, vmem_limit_bytes=62 * 1024 * 1024),
        name="ssm_backward",
    )(tokens, x, g, c.T, wt, a_log[None], dt_bias[None], d_skip[None])
    gx, gc, gp, gw = pl.pallas_call(
        store,
        out_shape=tuple(jax.ShapeDtypeStruct(r.shape, r.dtype) for r in results),
        in_specs=[pl.BlockSpec(memory_space=pl.ANY)] * 4,
        out_specs=(hbm,) * 4,
        scratch_shapes=[dma((4,))],
        name="store_results",
    )(*results)
    return (gx[None], gc.T[None], gp.T[None], gw.T)


def solution(mesh):
    in_specs = (
        P("dp", "ctx", None),
        P("dp", "ctx", None),
        P("dp", "ctx", None),
        P("dp", None),
        P(),
        P(),
        P(),
        P("dp", "ctx", None),
    )
    out_specs = (P("dp", "ctx", None), P("dp", "ctx", None), P("dp", "ctx", None), P("dp", "ctx"))
    return jax.shard_map(
        per_device, mesh=mesh, in_specs=in_specs, out_specs=out_specs, check_vma=False
    )
```

```python
import functools

import jax
import jax.numpy as jnp
from jax import lax
from jax.experimental import pallas as pl
from jax.experimental.pallas import tpu as pltpu
from jax.sharding import PartitionSpec as P

STATE = 64
LANES = 128
MESH = pl.DeviceIdType.MESH
F32 = jnp.float32
BF16 = jnp.bfloat16


def inner_group(n):
    b = 1
    while b * b < n and n % (2 * b) == 0:
        b *= 2
    return b


def up(n, m):
    return -(-n // m) * m


def dot(a, b):
    return jnp.dot(a, b, preferred_element_type=F32)


def dot_nt(a, b):
    return lax.dot_general(a, b, (((1,), (1,)), ((), ())), preferred_element_type=F32)


def split(v):
    hi = v.astype(BF16)
    return hi, (v - hi.astype(F32)).astype(BF16)


def dot_split(v, b):
    hi, lo = split(v)
    return dot(hi, b) + dot(lo, b)


def dot_exact(sel, v):
    hi, rest = v.astype(BF16), None
    rest = v - hi.astype(F32)
    mid, low = split(rest)
    return dot(sel, hi) + dot(sel, mid) + dot(sel, low)


def iota(shape, dim):
    return lax.broadcasted_iota(jnp.int32, shape, dim)


def kernel(cfg, tok_h, x_h, g_h, c, w_own, a_log, dt_bias, d_skip, gx_h, gc_h, gp_h, gw_h, gx, gc, gp, gw, w, vec, tok, x, g, wall, trecv, gall, sloc, crecv,
           dall, spread_m, gather_m, xw, gwt, dx, proj, cum_r, dt_r, cumt, rowt, qacc, ds, part, pst, precv, zst, zrecv,
           decs, decr, wzs, wzr, wfs, wfr, as_, ar, gzs, gzr, gfs, gfr, os, cs, cr, ps, pr, es, er, ms, mr, ls):
    n_dp, n_ctx, t, rows, heads, width, cols = cfg
    wide = rows % LANES == 0
    unroll = True
    halved = wide and rows % (n_ctx * LANES) == 0 and n_ctx == 2
    half = rows // n_ctx
    n_b = inner_group(n_dp)
    n_a = n_dp // n_b
    my_a, my_b = lax.div(lax.axis_index("dp"), n_b), lax.rem(lax.axis_index("dp"), n_b)
    loads = [pltpu.make_async_copy(src, dst, ls.at[i]) for i, (src, dst) in enumerate(((x_h, x), (g_h, g), (tok_h, tok)))]
    for load in loads:
        load.start()
    groups = x.shape[1] // LANES
    gh = LANES // width
    cb = cols // n_ctx
    cbp = up(cb, 16)
    me = lax.axis_index("dp")
    my = lax.axis_index("ctx")

    def peer(k):
        return lax.rem(me + k, n_dp)

    def mate(k):
        return lax.rem(my + k, n_ctx)

    def col(ref, i):
        return ref.at[:, pl.ds(pl.multiple_of(i * rows, LANES), rows)] if wide else ref.at[i]

    def blk(i):
        return pl.ds(pl.multiple_of(i * t, LANES), t)

    def lanes(q):
        return pl.ds(pl.multiple_of(q * LANES, LANES), LANES)

    barrier = pltpu.get_barrier_semaphore()

    def greet(k, carry):
        pl.semaphore_signal(barrier, inc=1, device_id=(peer(k), my), device_id_type=MESH)
        return carry

    def greet_mate(k, carry):
        pl.semaphore_signal(barrier, inc=1, device_id=(me, mate(k)), device_id_type=MESH)
        return carry

    lax.fori_loop(1, n_dp, greet, 0)
    lax.fori_loop(1, n_ctx, greet_mate, 0)
    pl.semaphore_wait(barrier, n_dp + n_ctx - 2)

    def origin(ka, kb):
        return lax.rem(my_a + n_a - ka, n_a) * n_b + lax.rem(my_b + n_b - kb, n_b)

    def w_slot(i):
        if halved:
            return wall.at[my, :, pl.ds(pl.multiple_of(i * half, LANES), half)]
        return col(wall, i)

    def g_slot(i):
        return gall.at[:, blk(lax.rem(i, n_b))]

    def far(slot, send, recv, ka):
        return pltpu.make_async_remote_copy(
            src_ref=slot(me), dst_ref=slot(me), send_sem=send.at[ka], recv_sem=recv.at[ka],
            device_id=(lax.rem(my_a + ka, n_a) * n_b + my_b, my), device_id_type=MESH)

    def near(slot, send, recv, ka, kb):
        i = origin(ka, 0)
        return pltpu.make_async_remote_copy(
            src_ref=slot(i), dst_ref=slot(i), send_sem=send.at[ka * n_b + kb], recv_sem=recv.at[ka * n_b + kb],
            device_id=(my_a * n_b + lax.rem(my_b + kb, n_b), my), device_id_type=MESH)

    def across(ka):
        i = lax.rem(my_a + n_a - ka, n_a) * n_b
        block = wall.at[my, :, pl.ds(pl.multiple_of(i * half, LANES), n_b * half)]
        return pltpu.make_async_remote_copy(
            src_ref=block, dst_ref=block, send_sem=ms.at[ka], recv_sem=mr.at[ka],
            device_id=(me, 1 - my), device_id_type=MESH)

    def a_copy(kb, a):
        b_to = lax.rem(my_b + kb, n_b)
        return pltpu.make_async_remote_copy(
            src_ref=col(tok, a * n_b + b_to), dst_ref=trecv.at[a, blk(my_b), :],
            send_sem=as_.at[kb * n_a + a], recv_sem=ar.at[kb * n_a + a],
            device_id=(my_a * n_b + b_to, my), device_id_type=MESH)

    def a_each(act):
        def one(a, carry):
            each(n_b, lambda kb: act(a_copy(kb, a)))
            return carry

        lax.fori_loop(0, n_a, one, 0)

    def z_copy(k):
        a_to = lax.rem(my_a + k, n_a)
        return pltpu.make_async_remote_copy(
            src_ref=zst.at[a_to], dst_ref=zrecv.at[my_a], send_sem=gzs.at[k], recv_sem=gzr.at[k],
            device_id=(a_to * n_b + my_b, my), device_id_type=MESH)

    def c_copy(k):
        other = mate(k)
        which = jnp.where(other > my, 0, 1)
        return pltpu.make_async_remote_copy(
            src_ref=sloc.at[which], dst_ref=crecv.at[my], send_sem=cs.at[k], recv_sem=cr.at[k],
            device_id=(me, other), device_id_type=MESH)

    def d_copy(k):
        return pltpu.make_async_remote_copy(
            src_ref=decs, dst_ref=decr.at[my], send_sem=es.at[k], recv_sem=er.at[k],
            device_id=(me, mate(k)), device_id_type=MESH)

    def p_copy(k):
        return pltpu.make_async_remote_copy(
            src_ref=pst.at[mate(k)], dst_ref=precv.at[my], send_sem=ps.at[k], recv_sem=pr.at[k],
            device_id=(me, mate(k)), device_id_type=MESH)

    def each(n, act):
        def step(k, carry):
            act(k)
            return carry

        lax.fori_loop(1, n, step, 0)

    def spread_near(slot, send, recv, ka):
        each(n_b, lambda kb: near(slot, send, recv, ka, kb).start())

    def first(slot, send, recv, fsend, frecv):
        each(n_a, lambda ka: far(slot, send, recv, ka).start())
        spread_near(slot, fsend, frecv, 0)

    def pass_on(slot, send, recv, fsend, frecv):
        def one(ka):
            far(slot, send, recv, ka).wait_recv()
            spread_near(slot, fsend, frecv, ka)

        each(n_a, one)

    def arrive(slot, fsend, frecv, ka):
        each(n_b, lambda kb: near(slot, fsend, frecv, ka, kb).wait_recv())

    def settle(slot, send, recv, fsend, frecv):
        each(n_a, lambda ka: far(slot, send, recv, ka).wait_send())

        def one(ka, carry):
            each(n_b, lambda kb: near(slot, fsend, frecv, ka, kb).wait_send())
            return carry

        lax.fori_loop(0, n_a, one, 0)

    inner = x.shape[1]
    wcols = w.shape[0]
    w[...] = jnp.zeros_like(w)
    w[:cols, :] = w_own[...]
    if halved:
        wall[my, :, pl.ds(pl.multiple_of(me * half, LANES), half)] = w[:, pl.ds(pl.multiple_of(my * half, LANES), half)]
    elif wide:
        wall[:, pl.ds(pl.multiple_of(me * rows, LANES), rows)] = w[...]
    else:
        wall[me] = w[...]
    first(w_slot, wzs, wzr, wfs, wfr)
    vec[...] = jnp.zeros_like(vec)
    for i, ref in enumerate((a_log, dt_bias, d_skip)):
        vec[i:i + 1, :heads] = ref[...]
    for load in loads:
        load.wait()
    pass_on(w_slot, wzs, wzr, wfs, wfr)
    a_each(lambda copy: copy.start())
    for a in range(n_a):
        trecv[a, blk(my_b), :] = col(tok, a * n_b + my_b)[...]
    proj[...] = jnp.zeros_like(proj)
    qacc[...] = jnp.zeros_like(qacc)
    ds[...] = jnp.zeros_like(ds)
    rowt[...] = jnp.zeros_like(rowt)
    spread_m[...] = jnp.where(iota((LANES, inner), 0) == iota((LANES, inner), 1) // width, 1.0, 0.0).astype(BF16)
    gather_m[...] = jnp.where(iota((inner, LANES), 1) == iota((inner, LANES), 0) // width, 1.0, 0.0).astype(BF16)
    head = iota((t, LANES), 1) // width

    def outer(q, carry):
        x4 = x[:, lanes(q)]
        zero = jnp.zeros_like(x4)
        xm = jnp.concatenate([jnp.where(head == j, x4, zero) for j in range(gh)], axis=0)
        dall[q] = dot_nt(xm, g[:, lanes(q)])
        return carry

    lax.fori_loop(0, groups, outer, 0)

    def land(ka, carry):
        arrive(w_slot, wfs, wfr, ka)
        if halved:
            across(ka).start()
        return carry

    lax.fori_loop(0, n_a, land, 0)
    if halved:
        lax.fori_loop(0, n_a, lambda ka, carry: (across(ka).wait_recv(), carry)[1], 0)
        total = None
        for k in range(n_ctx):
            picked = jnp.concatenate(
                [tok[:, i * rows + k * half:i * rows + (k + 1) * half] for i in range(n_dp)], axis=1)
            term = dot_nt(picked, wall[k])
            total = term if total is None else total + term
        proj[:, :wcols] = total
    elif wide:
        proj[:, :wcols] = dot_nt(tok[...], wall[...])
    else:
        def shard(i, carry):
            proj[:, :wcols] += dot_nt(tok[i], wall[i])
            return carry

        lax.fori_loop(0, n_dp, shard, 0)
    rate_scale = -jnp.exp(vec[0:1, :])
    b = proj[:, :STATE].astype(BF16)
    z = proj[:, STATE:STATE + LANES] + vec[1:2, :]
    dt = jnp.maximum(z, 0.0) + jnp.log1p(jnp.exp(-jnp.abs(z)))
    row_i, col_i = iota((t, t), 0), iota((t, t), 1)
    lower = jnp.where(row_i >= col_i, 1.0, 0.0).astype(BF16)
    upper = jnp.where(col_i >= row_i, 1.0, 0.0).astype(BF16)
    cum = dot_exact(lower, rate_scale * dt)
    cum_r[...] = cum
    dt_r[...] = dt
    cumt[...] = cum.T
    last = cum_r[t - 1:t, :]
    to_end = jnp.exp(last - cum)
    wgt = to_end * dt
    grow = jnp.exp(cum)
    w_bf = wgt.astype(BF16)
    e_bf = grow.astype(BF16)
    ct = c[...]
    bt = b.astype(F32).T.astype(BF16)
    cv = ct.astype(F32).T.astype(BF16)
    skip_hi, skip_lo = split(vec[...])

    span = [slice(q * LANES, (q + 1) * LANES) for q in range(groups)]
    for at in span:
        xw[:, at] = (dot(w_bf, spread_m[:, at]) * x[:, at].astype(F32)).astype(BF16)
        gwt[:, at] = (dot(e_bf, spread_m[:, at]) * g[:, at].astype(F32)).astype(BF16)
    sloc[0] = dot(bt, xw[...]).astype(BF16)
    sloc[1] = dot(ct, gwt[...]).astype(BF16)
    each(n_ctx, lambda k: c_copy(k).start())
    if n_ctx > 2:
        decs[...] = jnp.broadcast_to(jnp.exp(last), decs.shape)
        crecv[my] = jnp.zeros(crecv.shape[1:], BF16)
        decr[my] = jnp.zeros(decr.shape[1:], F32)
        each(n_ctx, lambda k: d_copy(k).start())

    scores = dot_nt(b, cv)
    causal = col_i >= row_i

    def mix(q, carry):
        g4 = g[:, lanes(q)]
        shift = lax.rem(LANES - gh * q, LANES)
        cum_s = pltpu.roll(cum_r[...], shift, 1)
        dt_s = pltpu.roll(dt_r[...], shift, 1)
        total = ds[...]
        quot = qacc[...]
        mixed = []
        for j in range(gh):
            h = gh * q + j
            spread = cumt[pl.ds(h, 1), :] - cum_s[:, j:j + 1]
            factor = jnp.exp(jnp.where(causal, spread, -1e30))
            step = dt_s[:, j:j + 1]
            d = dall[q, j * t:(j + 1) * t]
            fs = factor * scores
            mixed.append((fs * step).astype(BF16))
            u = d * fs
            quot = jnp.where(col_i == h, jnp.sum(u, axis=1, keepdims=True), quot)
            rowt[pl.ds(h, 1), :] = jnp.sum(u * step, axis=0, keepdims=True)
            total = total + d * (factor * step)
        ds[...] = total
        qacc[...] = quot
        out = dot(jnp.concatenate(mixed, axis=0), g4)
        skip = dot(skip_hi, spread_m[:, lanes(q)]) + dot(skip_lo, spread_m[:, lanes(q)])
        acc = skip[2:3] * g4.astype(F32)
        for j in range(gh):
            acc = acc + jnp.where(head == j, out[j * t:(j + 1) * t], 0.0)
        dx[:, lanes(q)] = acc
        return carry

    lax.fori_loop(0, groups, mix, 0, unroll=unroll)
    each(n_ctx, lambda k: c_copy(k).wait_recv())
    if n_ctx > 2:
        each(n_ctx, lambda k: d_copy(k).wait_recv())

    sv = sg = jnp.zeros((t, LANES), F32)
    db2 = dc2 = jnp.zeros((t, STATE), F32)
    gs = jnp.zeros((8, LANES), F32)
    for at in span:
        e, et = spread_m[:, at], gather_m[at, :]
        if n_ctx == 2:
            got = crecv[1 - my, :, at]
            none = jnp.zeros_like(got)
            s4 = jnp.where(my > 0, got, none)
            g4s = jnp.where(my < 1, got, none)
        else:
            s = jnp.zeros((STATE, LANES), F32)
            k = s
            for i in range(n_ctx):
                dec = dot_split(decr[i], e)[0:1]
                s = jnp.where(i < my, dec * s + crecv[i, :, at].astype(F32), s)
            for i in reversed(range(n_ctx)):
                dec = dot_split(decr[i], e)[0:1]
                k = jnp.where(i > my, dec * k + crecv[i, :, at].astype(F32), k)
            s4, g4s = s.astype(BF16), k.astype(BF16)
            both = jnp.sum(s * k, axis=0, keepdims=True)
            gs = gs + dot_split(jnp.broadcast_to(both, (8, LANES)), et)
        us = dot(cv, s4)
        ug = dot(b, g4s)
        sv = sv + dot_split(x[:, at].astype(F32) * ug, et)
        sg = sg + dot_split(g[:, at].astype(F32) * us, et)
        db2 = db2 + dot_nt(xw[:, at], g4s)
        dc2 = dc2 + dot_nt(gwt[:, at], s4)
        gx[:, at] = (dx[:, at] + dot(w_bf, e) * ug).astype(BF16)
    stores = [pltpu.make_async_copy(src, dst, os.at[i]) for i, (src, dst) in enumerate(
        ((gx, gx_h), (gc, gc_h), (gp, gp_h), (gw, gw_h)))]
    stores[0].start()
    dsv = ds[...]
    db = dot_split(dsv, cv) + db2
    dc = dot_split(dsv.T, b) + dc2
    gc[...] = dc.T.astype(BF16)
    stores[1].start()
    quot = qacc[...]
    v = sv
    vw = v * wgt
    dcum = rowt[...].T + grow * sg - dt * quot - vw
    tail = jnp.sum(vw, axis=0, keepdims=True)
    if n_ctx > 2:
        tail = tail + jnp.exp(last) * gs[0:1, :]
    dcum = dcum + jnp.where(row_i == t - 1, tail, 0.0)
    drate = dot_exact(upper, dcum)
    ddt = quot + v * to_end + rate_scale * drate
    dz = ddt / (1.0 + jnp.exp(-z))
    proj[...] = jnp.zeros_like(proj)
    proj[:, :STATE] = db.astype(BF16).astype(F32)
    proj[:, STATE:cols] = dz[:, :heads]
    whole = proj[...]
    turned = whole.T[:wcols].astype(BF16)
    gall[:, blk(my_b)] = turned
    spread_near(g_slot, gfs, gfr, 0)
    gp[...] = turned[:cols]
    stores[2].start()
    part[...] = jnp.zeros_like(part)
    a_each(lambda copy: copy.wait_recv())
    arrive(g_slot, gfs, gfr, 0)
    for a in range(n_a):
        part[a, :wcols] = dot(gall[...], trecv[a])
        for o in range(n_ctx):
            pst[o, a] = part[a, o * cb:o * cb + cbp, :].astype(BF16)
    each(n_ctx, lambda k: p_copy(k).start())
    each(n_ctx, lambda k: p_copy(k).wait_recv())

    for a in range(n_a):
        zst[a] = lax.fori_loop(
            1, n_ctx, lambda k, acc: acc + precv[mate(k), a].astype(F32), pst[my, a].astype(F32)).astype(BF16)
    each(n_a, lambda k: z_copy(k).start())
    each(n_a, lambda k: z_copy(k).wait_recv())
    total = lax.fori_loop(
        1, n_a, lambda k, acc: acc + zrecv[lax.rem(my_a + k, n_a)].astype(F32), zst[my_a].astype(F32))
    gw[...] = (total * (1.0 / n_dp))[:cb]
    stores[3].start()
    settle(w_slot, wzs, wzr, wfs, wfr)
    if halved:
        lax.fori_loop(0, n_a, lambda ka, carry: (across(ka).wait_send(), carry)[1], 0)
    a_each(lambda copy: copy.wait_send())
    each(n_b, lambda kb: near(g_slot, gfs, gfr, 0, kb).wait_send())
    each(n_a, lambda k: z_copy(k).wait_send())
    for copy in stores:
        copy.wait()
    each(n_ctx, lambda k: c_copy(k).wait_send())
    each(n_ctx, lambda k: p_copy(k).wait_send())
    if n_ctx > 2:
        each(n_ctx, lambda k: d_copy(k).wait_send())


def store(*refs):
    held, sems = refs[8:12], refs[-1]
    loads = [pltpu.make_async_copy(refs[i], held[i], sems.at[0, i]) for i in range(4)]
    copies = [pltpu.make_async_copy(held[i], refs[4 + i], sems.at[1, i]) for i in range(4)]
    for load in loads:
        load.start()
    for load, copy in zip(loads, copies):
        load.wait()
        copy.start()
    for copy in copies:
        copy.wait()


def per_device(layer_in, inner_act, readout, w_in, a_log, dt_bias, d_skip, grad_out):
    n_dp, n_ctx = lax.axis_size("dp"), lax.axis_size("ctx")
    tokens, x, c, g = layer_in[0], inner_act[0], readout[0], grad_out[0]
    t, inner = x.shape
    rows, cols = w_in.shape
    heads = a_log.shape[0]
    width = inner // heads
    wcols = up(cols, 16)
    wide = rows % LANES == 0
    wt = w_in.T
    if not wide:
        tokens = jnp.swapaxes(tokens.reshape(t, n_dp, rows), 0, 1)
    cb = cols // n_ctx
    cbp = up(cb, 16)
    part_rows = up(max(wcols, cols - cb + cbp), 8)
    vm = pltpu.VMEM
    n_a = n_dp // inner_group(n_dp)
    if not wide:
        wall = (n_dp, wcols, rows)
    elif rows % (n_ctx * LANES) == 0 and n_ctx == 2:
        wall = (n_ctx, wcols, n_dp * rows // n_ctx)
    else:
        wall = (wcols, n_dp * rows)
    shapes = (
        jax.ShapeDtypeStruct((t, inner), BF16),
        jax.ShapeDtypeStruct((STATE, t), BF16),
        jax.ShapeDtypeStruct((cols, t), BF16),
        jax.ShapeDtypeStruct((cb, rows), F32),
    )
    n_b = inner_group(n_dp)
    scratch = [vm(r.shape, r.dtype) for r in shapes] + [
        vm((wcols, rows), BF16),
        vm((8, LANES), F32),
        vm(tokens.shape, BF16),
        vm((t, inner), BF16),
        vm((t, inner), BF16),
        vm(wall, BF16),
        vm((n_a, n_b * t, rows), BF16),
        vm((wcols, n_b * t), BF16),
        vm((2, STATE, inner), BF16),
        vm((n_ctx, STATE, inner), BF16),
        vm((inner // LANES, LANES // width * t, t), F32),
        vm((LANES, inner), BF16),
        vm((inner, LANES), BF16),
        vm((t, inner), BF16),
        vm((t, inner), BF16),
        vm((t, inner), F32),
        vm((t, 2 * LANES), F32),
        vm((t, LANES), F32),
        vm((t, LANES), F32),
        vm((LANES, t), F32),
        vm((LANES, t), F32),
        vm((t, LANES), F32),
        vm((t, t), F32),
        vm((n_a, part_rows, rows), F32),
        vm((n_ctx, n_a, cbp, rows), BF16),
        vm((n_ctx, n_a, cbp, rows), BF16),
        vm((n_a, cbp, rows), BF16),
        vm((n_a, cbp, rows), BF16),
        vm((8, LANES), F32),
        vm((n_ctx, 8, LANES), F32),
    ]
    dma = pltpu.SemaphoreType.DMA
    scratch += [dma((n_a,))] * 2 + [dma((n_dp,))] * 4 + [dma((n_a,))] * 2 + [dma((n_dp,))] * 2 + [dma((4,))]
    scratch += [dma((n_ctx,))] * 6 + [dma((n_a,))] * 2 + [dma((3,))]
    hbm = pl.BlockSpec(memory_space=pltpu.HBM)
    spec = pl.BlockSpec(memory_space=pltpu.VMEM)
    cfg = (n_dp, n_ctx, t, rows, heads, width, cols)
    results = pl.pallas_call(
        functools.partial(kernel, cfg),
        out_shape=shapes,
        in_specs=[hbm] * 3 + [spec] * 5,
        out_specs=(hbm,) * 4,
        scratch_shapes=scratch,
        compiler_params=pltpu.CompilerParams(
            collective_id=0, has_side_effects=True, vmem_limit_bytes=62 * 1024 * 1024),
        name="ssm_backward",
    )(tokens, x, g, c.T, wt, a_log[None], dt_bias[None], d_skip[None])
    gx, gc, gp, gw = pl.pallas_call(
        store,
        out_shape=tuple(jax.ShapeDtypeStruct(r.shape, r.dtype) for r in results),
        in_specs=[pl.BlockSpec(memory_space=pl.ANY)] * 4,
        out_specs=(hbm,) * 4,
        scratch_shapes=[vm(r.shape, r.dtype) for r in shapes] + [dma((2, 4))],
        name="store_results",
    )(*results)
    return (gx[None], gc.T[None], gp.T[None], gw.T)


def solution(mesh):
    in_specs = (
        P("dp", "ctx", None),
        P("dp", "ctx", None),
        P("dp", "ctx", None),
        P("dp", None),
        P(),
        P(),
        P(),
        P("dp", "ctx", None),
    )
    out_specs = (P("dp", "ctx", None), P("dp", "ctx", None), P("dp", "ctx", None), P("dp", "ctx"))
    return jax.shard_map(
        per_device, mesh=mesh, in_specs=in_specs, out_specs=out_specs, check_vma=False
    )
```
